32 devices in a mesh: dp: 4 (over x, core), wide: 8 (over z, y).
Axes of the slice: x: 2, y: 2, z: 4, core: 2. Of those that a mesh axis runs over, the one named last changes fastest.
Arguments:
- inputs: bfloat16 [512, 1024], P('dp', 'wide'), may hold values from -6 to 6
- cotangent: bfloat16 [512, 4096], P('dp', 'wide'), may hold values from -3 to 3
- up_blocks: bfloat16 [4, 128, 4096], P(None, None, 'wide'), may hold values from -0.25 to 0.25
- block_links: int32 [4, 16], P(None, 'wide'), may hold values 0 or 1
- rank_down: bfloat16 [1024, 256], P('wide'), may hold values from -0.1875 to 0.1875
- rank_up: bfloat16 [256, 4096], P(None, 'wide'), may hold values from -0.375 to 0.375
Outputs:
- hidden: bfloat16 [512, 4096], P('dp', 'wide')
- input_grad: bfloat16 [512, 1024], P('dp', 'wide')
- block_grad: bfloat16 [4, 128, 4096], P(None, None, 'wide')
- up_grad: bfloat16 [256, 4096], P(None, 'wide')
- down_grad: bfloat16 [1024, 256], P('wide')
The draws below stay inside these ranges and needn't reach their ends.
All inputs are finite; a program needn't handle non-finite values. No bound on the sum of `block_links` on one device may be relied on, other than what follows from the above.
Results may differ from the reference program's by a relative error of at most 0.006.
Values may be sent and summed in bfloat16 or wider, within the bound.
A program may use at most 64 MiB of HBM per device.

```python
import math
import jax
import jax.numpy as jnp

BLOCK = 256
RANK = 256
XW = 128
HW = 512
L1 = 4
D = 1024
H = 4096
HB = 16
TOKENS = 512
N_WIDE = 8


def place_ends(entries, own_key, smallest, high):
    longest = entries.shape.index(max(entries.shape))
    spots = []
    for shift in (0, 1):
        where = [jax.random.randint(jax.random.fold_in(own_key, axis), (), 0, length) for axis, length in enumerate(entries.shape)]
        where[longest] = (where[longest] + shift) % entries.shape[longest]
        spots.append(tuple(where))
    return entries.at[spots[0]].set(smallest).at[spots[1]].set(high)


def level_of(own_key, dims, cuts, least, high):
    def one(position, parts):
        steps = jax.random.uniform(jax.random.fold_in(jax.random.fold_in(own_key, 6), position), (parts,), jnp.float32, least / len(cuts), high / len(cuts))
        return jnp.repeat(jnp.exp(steps), dims[position] // parts).reshape((-1,) + (1,) * (len(dims) - position - 1))

    factor_of = one(*cuts[0])
    for cut in cuts[1:]:
        factor_of = factor_of * one(*cut)
    return factor_of


def normal_values(key, dims, scale, bound, shards=(), kind=jnp.bfloat16):
    gain = level_of(key, dims, shards, -0.22, 0.18) if shards else 1.0
    entries = jax.random.normal(key, dims, jnp.float32) * scale * gain
    return jnp.minimum(jnp.maximum(entries, -bound), bound).astype(kind)


def setup_inputs(seed: int = 0) -> dict:
    key_of = jax.random.split(jax.random.key(seed), 7)
    return {
        "inputs": normal_values(key_of[0], (TOKENS, D), 1.0, 6.0, ((0, 4), (1, 8))),
        "cotangent": normal_values(key_of[1], (TOKENS, H), 0.5, 3.0, ((0, 4), (1, 8))),
        "up_blocks": normal_values(key_of[2], (L1, XW, H), (L1 * XW) ** -0.5, 0.25, ((2, 8),)),
        "block_links": place_ends((jax.random.randint(key_of[3], (L1, HB), 0, 4) < 3).astype(jnp.int32), jax.random.fold_in(key_of[3], 1), 0, 1),
        "rank_down": normal_values(key_of[4], (D, RANK), D ** -0.5, 0.1875, ((0, 8),)),
        "rank_up": normal_values(key_of[5], (RANK, H), RANK ** -0.5, 0.375, ((1, 8),)),
    }


def partner_of(groups, level_index):
    if level_index == 0:
        return groups
    return jnp.bitwise_xor(groups, 2 ** (level_index - 1))

def reference(inputs, cotangent, up_blocks, block_links, rank_down, rank_up):
    groups = jnp.arange(N_WIDE, dtype=jnp.int32)
    column_mask = jnp.repeat(block_links, BLOCK, axis=1).astype(jnp.float32)
    latent = jnp.dot(inputs, rank_down, preferred_element_type=jnp.float32).astype(jnp.bfloat16)
    preact = jnp.dot(latent, rank_up, preferred_element_type=jnp.float32)
    grouped = inputs.astype(jnp.float32).reshape(TOKENS, N_WIDE, XW)
    for level_index in range(L1):
        partner = grouped[:, partner_of(groups, level_index), :]
        weights = up_blocks[level_index].astype(jnp.float32).reshape(XW, N_WIDE, HW)
        product = jnp.einsum('tgi,igh->tgh', partner, weights).reshape(TOKENS, H)
        preact = preact + column_mask[level_index] * product
    hidden = jax.nn.silu(preact).astype(jnp.bfloat16)
    sigmoid_value = jax.nn.sigmoid(preact)
    slope = sigmoid_value * (1.0 + preact * (1.0 - sigmoid_value))
    grad_pre = (cotangent.astype(jnp.float32) * slope).astype(jnp.bfloat16)
    mid = jnp.dot(grad_pre, rank_up.T, preferred_element_type=jnp.float32).astype(jnp.bfloat16)
    input_acc = jnp.dot(mid, rank_down.T, preferred_element_type=jnp.float32)
    grad_grouped = grad_pre.astype(jnp.float32).reshape(TOKENS, N_WIDE, HW)
    block_list = []
    for level_index in range(L1):
        partner_index = partner_of(groups, level_index)
        masked = grad_grouped * column_mask[level_index].reshape(N_WIDE, HW)
        weights = up_blocks[level_index].astype(jnp.float32).reshape(XW, N_WIDE, HW)
        contrib = jnp.einsum('tgh,igh->tgi', masked, weights)
        input_acc = input_acc + contrib[:, partner_index, :].reshape(TOKENS, D)
        partner = grouped[:, partner_index, :]
        block_list.append(jnp.einsum('tgi,tgh->igh', partner, masked).reshape(XW, H))
    grad_scale = 1.0 / math.sqrt(TOKENS)
    block_grad = (grad_scale * jnp.stack(block_list)).astype(jnp.bfloat16)
    up_grad = (grad_scale * jnp.dot(latent.T, grad_pre, preferred_element_type=jnp.float32)).astype(jnp.bfloat16)
    down_grad = (grad_scale * jnp.dot(inputs.T, mid, preferred_element_type=jnp.float32)).astype(jnp.bfloat16)
    input_grad = input_acc.astype(jnp.bfloat16)
    return (hidden, input_grad, block_grad, up_grad, down_grad)
```

```python
import functools
import math

import jax
import jax.numpy as jnp
from jax import lax
from jax.experimental import pallas as pl
from jax.experimental.pallas import tpu as pltpu
from jax.sharding import PartitionSpec as P


def partner(shard, axis, distance):
    return lax.ppermute(shard, axis, [(i, i ^ 1 << distance) for i in range(lax.axis_size(axis))])


def fetch_partner(values, bit_index):
    return partner(values, "wide", bit_index)


def return_partner(values, bit_index):
    return partner(values, "wide", bit_index)


def gram_product(left, right):
    return lax.dot_general(
        left, right, (((0,), (0,)), ((), ())), preferred_element_type=jnp.float32
    )


def right_transpose(left, right):
    return lax.dot_general(
        left, right, (((1,), (1,)), ((), ())), preferred_element_type=jnp.float32
    )


def on_device(inputs, cotangent, up_blocks, block_links, rank_down, rank_up):
    width_count = lax.axis_size("wide")
    levels = min(6, 3 + 3 * (width_count // 64))
    tokens_all = inputs.shape[0] * lax.axis_size("dp")
    grad_scale = 1.0 / math.sqrt(tokens_all)
    block_cols = up_blocks.shape[2] // block_links.shape[1]
    column_mask = jnp.repeat(block_links, block_cols, axis=1).astype(jnp.bfloat16)
    latent_part = jnp.dot(inputs, rank_down, preferred_element_type=jnp.float32)
    latent = lax.psum(latent_part, "wide").astype(jnp.bfloat16)
    pieces = [inputs] + [fetch_partner(inputs, bit_index) for bit_index in range(levels)]
    preact = jnp.dot(latent, rank_up, preferred_element_type=jnp.float32)
    for level_index in range(levels + 1):
        product = jnp.dot(
            pieces[level_index], up_blocks[level_index], preferred_element_type=jnp.float32
        )
        preact = preact + column_mask[level_index].astype(jnp.float32) * product
    hidden = jax.nn.silu(preact).astype(jnp.bfloat16)
    sigmoid_value = jax.nn.sigmoid(preact)
    slope = sigmoid_value * (1.0 + preact * (1.0 - sigmoid_value))
    grad_pre = (cotangent.astype(jnp.float32) * slope).astype(jnp.bfloat16)
    mid_part = right_transpose(grad_pre, rank_up)
    mid = lax.psum(mid_part, "wide").astype(jnp.bfloat16)
    input_acc = right_transpose(mid, rank_down)
    block_terms = []
    for level_index in range(levels + 1):
        masked = grad_pre * column_mask[level_index]
        contrib = right_transpose(masked, up_blocks[level_index])
        if level_index == 0:
            input_acc = input_acc + contrib
        else:
            input_acc = input_acc + return_partner(contrib, level_index - 1)
        level_term = gram_product(pieces[level_index], masked)
        block_terms.append(level_term)
    stacked = jnp.stack(block_terms)
    up_term = gram_product(latent, grad_pre)
    down_term = gram_product(inputs, mid)
    stacked, up_term, down_term = lax.psum((stacked, up_term, down_term), "dp")
    block_grad = (grad_scale * stacked).astype(jnp.bfloat16)
    up_grad = (grad_scale * up_term).astype(jnp.bfloat16)
    down_grad = (grad_scale * down_term).astype(jnp.bfloat16)
    input_grad = input_acc.astype(jnp.bfloat16)
    return (hidden, input_grad, block_grad, up_grad, down_grad)


CHUNK_ROWS = 16
MESH = pl.DeviceIdType.MESH


def fused_kernel(
    dims, x_in, cot_in, blocks_in, links, down_in, up_in,
    hidden_out, input_out, block_out, up_out, down_out,
    pieces, latent, grads, mid, weights, down, cot, blocks,
    part, part_send, sums, hidden, base, contrib_send, contrib_got,
    input_grad, block_grad, up_grad, down_grad,
    send_sem, recv_sem, local_sem,
):
    width, copies, levels, scale = dims
    tokens, features = x_in.shape
    rank = down_in.shape[1]
    units = up_in.shape[1]
    block_cols = units // links.shape[1]
    me_w, me_d = lax.axis_index("wide"), lax.axis_index("dp")
    count = [0, 0]
    pending = []

    def load(source, target):
        copy = pltpu.make_async_copy(source, target, local_sem.at[count[0]])
        count[0] += 1
        copy.start()
        return copy

    def push(source, target, wide=None, dp=None):
        where = {"wide": me_w if wide is None else wide, "dp": me_d if dp is None else dp}
        copy = pltpu.make_async_remote_copy(
            src_ref=source, dst_ref=target,
            send_sem=send_sem.at[count[1]], recv_sem=recv_sem.at[count[1]],
            device_id=(where["dp"], where["wide"]), device_id_type=MESH,
        )
        count[1] += 1
        copy.start()
        pending.append(copy)
        return copy

    def rows(index, size=tokens):
        if isinstance(index, int):
            return pl.ds(index * size, size)
        return pl.ds(pl.multiple_of(index * size, size), size)

    get_x = load(x_in, pieces.at[0, rows(0)])
    get_down = load(down_in, down)
    get_up = load(up_in, weights.at[pl.ds(0, rank)])
    get_blocks = load(blocks_in, blocks)
    get_cot = load(cot_in, cot)

    barrier = pltpu.get_barrier_semaphore()
    for offset in range(1, width):
        pl.semaphore_signal(
            barrier, inc=1, device_id=(me_d, me_w ^ offset), device_id_type=MESH
        )
    for offset in range(1, copies):
        pl.semaphore_signal(
            barrier, inc=1, device_id=(me_d ^ offset, me_w), device_id_type=MESH
        )

    far_first = list(range(width - 1, 0, -1))
    near_first = list(range(1, width))
    own_rows = rows(me_w, CHUNK_ROWS)

    def scatter(turn, value):
        part[...] = value
        part_send[turn] = value.astype(jnp.bfloat16)

    def scatter_push(turn):
        return {
            offset: push(
                part_send.at[turn, rows(me_w ^ offset, CHUNK_ROWS)], sums.at[turn, offset],
                wide=me_w ^ offset,
            )
            for offset in far_first
        }

    def reduce_chunk(turn, arriving):
        total = part[own_rows, :]
        for offset in near_first:
            arriving[offset].wait_recv()
            total = total + sums[turn, offset].astype(jnp.float32)
        return total.astype(jnp.bfloat16)

    def gather_push(buffer):
        return {
            offset: push(buffer.at[own_rows], buffer.at[own_rows], wide=me_w ^ offset)
            for offset in far_first
        }

    get_x.wait()
    get_down.wait()
    x = pieces[0, 0:tokens, :]
    scatter(0, jnp.dot(x, down[...], preferred_element_type=jnp.float32))
    pl.semaphore_wait(barrier, width - 1 + copies - 1)
    latent_parts = scatter_push(0)
    fetched = [
        push(pieces.at[0, rows(0)], pieces.at[level, rows(0)], wide=me_w ^ (1 << (level - 1)))
        for level in range(1, levels + 1)
    ]
    across, aside = {}, {}

    def spread(name, buffer_slot):
        aside[name] = push(buffer_slot(0), buffer_slot(1), dp=me_d ^ 1)
        across[name] = push(buffer_slot(0), buffer_slot(2), dp=me_d ^ 2)

    def relay(name, buffer_slot):
        across[name].wait_recv()
        return push(buffer_slot(2), buffer_slot(3), dp=me_d ^ 1)

    def piece_slot(level):
        return lambda slot: pieces.at[level, rows(slot)]

    def latent_slot(slot):
        return latent.at[rows(slot)]

    def grads_slot(slot):
        return grads.at[rows(slot)]

    spread(("piece", 0), piece_slot(0))

    get_blocks.wait()
    for level in range(levels + 1):
        for block in range(links.shape[1]):
            cols = pl.ds(block * block_cols, block_cols)
            keep = links[level, block].astype(jnp.float32).astype(jnp.bfloat16)
            weights[pl.ds(rank + level * features, features), cols] = (
                blocks[level, :, cols] * keep
            )

    latent[own_rows, :] = reduce_chunk(0, latent_parts)
    latent_got = gather_push(latent)

    get_up.wait()
    for level in range(1, levels + 1):
        fetched[level - 1].wait_recv()
        spread(("piece", level), piece_slot(level))
    own_pieces = jnp.concatenate(
        [pieces[level, 0:tokens, :] for level in range(levels + 1)], axis=1
    )
    base[...] = jnp.dot(own_pieces, weights[rank:, :], preferred_element_type=jnp.float32)
    get_cot.wait()

    for offset in near_first:
        latent_got[offset].wait_recv()
    spread("latent", latent_slot)
    preact = base[...] + jnp.dot(
        latent[0:tokens, :], weights[0:rank, :], preferred_element_type=jnp.float32
    )
    sig = 1.0 / (1.0 + jnp.exp(-preact))
    slope = sig * (1.0 + preact * (1.0 - sig))
    grad_pre = (cot[...].astype(jnp.float32) * slope).astype(jnp.bfloat16)
    grads[0:tokens, :] = grad_pre
    hidden[...] = (preact * sig).astype(jnp.bfloat16)

    def back(lo, hi):
        return lax.dot_general(
            grads[0:tokens, :], weights[lo:hi, :], (((1,), (1,)), ((), ())),
            preferred_element_type=jnp.float32,
        )

    scatter(1, back(0, rank))
    mid_parts = scatter_push(1)
    spread("grads", grads_slot)
    contrib = back(rank, rank + (levels + 1) * features)
    returned = []
    for level in range(1, levels + 1):
        contrib_send[level - 1] = contrib[:, level * features:(level + 1) * features].astype(
            jnp.bfloat16
        )
        returned.append(
            push(
                contrib_send.at[level - 1], contrib_got.at[level - 1],
                wide=me_w ^ (1 << (level - 1)),
            )
        )
    base[:, 0:features] = contrib[:, 0:features]
    outs = [load(hidden, hidden_out)]

    relayed = [relay(("piece", level), piece_slot(level)) for level in range(levels + 1)]
    relayed.append(relay("latent", latent_slot))

    mid[own_rows, :] = reduce_chunk(1, mid_parts)
    mid_got = gather_push(mid)
    mid_spread = []

    def spread_chunk(offset):
        owner = me_w ^ offset
        for slot in range(1, copies):
            chunk = rows(owner, CHUNK_ROWS)
            target = pl.ds(
                pl.multiple_of(slot * tokens + owner * CHUNK_ROWS, CHUNK_ROWS), CHUNK_ROWS
            )
            mid_spread.append(push(mid.at[chunk], mid.at[target], dp=me_d ^ slot))

    spread_chunk(0)
    relayed.append(relay("grads", grads_slot))

    def gram(left, right):
        return lax.dot_general(
            left, right, (((0,), (0,)), ((), ())), preferred_element_type=jnp.float32
        )

    for copy in aside.values():
        copy.wait_recv()
    for copy in relayed:
        copy.wait_recv()
    up_grad[...] = (scale * gram(latent[...], grads[...])).astype(jnp.bfloat16)
    outs.append(load(up_grad, up_out))
    for level in range(levels + 1):
        term = scale * gram(pieces[level], grads[...])
        for block in range(links.shape[1]):
            cols = slice(block * block_cols, (block + 1) * block_cols)
            keep = links[level, block].astype(jnp.float32)
            block_grad[level, :, cols] = (term[:, cols] * keep).astype(jnp.bfloat16)
        outs.append(load(block_grad.at[level], block_out.at[level]))

    for offset in near_first:
        mid_got[offset].wait_recv()
        spread_chunk(offset)
    total = base[:, 0:features] + lax.dot_general(
        mid[0:tokens, :], down[...], (((1,), (1,)), ((), ())),
        preferred_element_type=jnp.float32,
    )
    for level in range(levels):
        returned[level].wait_recv()
        total = total + contrib_got[level].astype(jnp.float32)
    input_grad[...] = total.astype(jnp.bfloat16)
    outs.append(load(input_grad, input_out))
    for copy in mid_spread:
        copy.wait_recv()
    down_grad[...] = (scale * gram(pieces[0], mid[...])).astype(jnp.bfloat16)
    outs.append(load(down_grad, down_out))
    for copy in pending:
        copy.wait_send()
    for copy in outs:
        copy.wait()


def fused(inputs, cotangent, up_blocks, block_links, rank_down, rank_up):
    width, copies = lax.axis_size("wide"), lax.axis_size("dp")
    tokens, features = inputs.shape
    level_count = up_blocks.shape[0]
    rank, units = rank_up.shape
    scale = 1.0 / math.sqrt(tokens * copies)
    levels = level_count - 1
    remote = 4 * (width - 1) + 2 * levels + 3 * (levels + 1) + 6 + 3 * width
    half, full = jnp.bfloat16, jnp.float32
    shapes = (
        ((tokens, units), half), ((tokens, features), half), (up_blocks.shape, half),
        ((rank, units), half), ((features, rank), half),
    )
    anywhere = pl.BlockSpec(memory_space=pl.ANY)
    return pl.pallas_call(
        functools.partial(fused_kernel, (width, copies, levels, scale)),
        out_shape=[jax.ShapeDtypeStruct(*entry) for entry in shapes],
        in_specs=[anywhere] * 3 + [pl.BlockSpec(memory_space=pltpu.SMEM)] + [anywhere] * 2,
        out_specs=[anywhere] * 5,
        scratch_shapes=[
            pltpu.VMEM((level_count, copies * tokens, features), half),
            pltpu.VMEM((copies * tokens, rank), half),
            pltpu.VMEM((copies * tokens, units), half),
            pltpu.VMEM((copies * tokens, rank), half),
            pltpu.VMEM((rank + level_count * features, units), half),
            pltpu.VMEM((features, rank), half),
            pltpu.VMEM((tokens, units), half),
            pltpu.VMEM(up_blocks.shape, half),
            pltpu.VMEM((tokens, rank), full),
            pltpu.VMEM((2, tokens, rank), half),
            pltpu.VMEM((2, width, CHUNK_ROWS, rank), half),
            pltpu.VMEM((tokens, units), half),
            pltpu.VMEM((tokens, units), full),
            pltpu.VMEM((levels, tokens, features), half),
            pltpu.VMEM((levels, tokens, features), half),
            pltpu.VMEM((tokens, features), half),
            pltpu.VMEM(up_blocks.shape, half),
            pltpu.VMEM((rank, units), half),
            pltpu.VMEM((features, rank), half),
            pltpu.SemaphoreType.DMA((remote,)),
            pltpu.SemaphoreType.DMA((remote,)),
            pltpu.SemaphoreType.DMA((9 + level_count,)),
        ],
        compiler_params=pltpu.CompilerParams(collective_id=0, has_side_effects=True),
    )(inputs, cotangent, up_blocks, block_links, rank_down, rank_up)


def choose(inputs, *others):
    fits = inputs.shape[0] == CHUNK_ROWS * lax.axis_size("wide") and lax.axis_size("dp") == 4
    return (fused if fits else on_device)(inputs, *others)


def solution(mesh):
    in_specs = (
        P("dp", "wide"),
        P("dp", "wide"),
        P(None, None, "wide"),
        P(None, "wide"),
        P("wide", None),
        P(None, "wide"),
    )
    out_specs = (
        P("dp", "wide"),
        P("dp", "wide"),
        P(None, None, "wide"),
        P(None, "wide"),
        P("wide", None),
    )
    return jax.shard_map(
        choose, mesh=mesh, in_specs=in_specs, out_specs=out_specs, check_vma=False
    )
```

```python
import functools
import math

import jax
import jax.numpy as jnp
from jax import lax
from jax.experimental import pallas as pl
from jax.experimental.pallas import tpu as pltpu
from jax.sharding import PartitionSpec as P


def partner(shard, axis, distance):
    return lax.ppermute(shard, axis, [(i, i ^ 1 << distance) for i in range(lax.axis_size(axis))])


def fetch_partner(values, bit_index):
    return partner(values, "wide", bit_index)


def return_partner(values, bit_index):
    return partner(values, "wide", bit_index)


def gram_product(left, right):
    return lax.dot_general(
        left, right, (((0,), (0,)), ((), ())), preferred_element_type=jnp.float32
    )


def right_transpose(left, right):
    return lax.dot_general(
        left, right, (((1,), (1,)), ((), ())), preferred_element_type=jnp.float32
    )


def on_device(inputs, cotangent, up_blocks, block_links, rank_down, rank_up):
    width_count = lax.axis_size("wide")
    levels = min(6, 3 + 3 * (width_count // 64))
    tokens_all = inputs.shape[0] * lax.axis_size("dp")
    grad_scale = 1.0 / math.sqrt(tokens_all)
    block_cols = up_blocks.shape[2] // block_links.shape[1]
    column_mask = jnp.repeat(block_links, block_cols, axis=1).astype(jnp.bfloat16)
    latent_part = jnp.dot(inputs, rank_down, preferred_element_type=jnp.float32)
    latent = lax.psum(latent_part, "wide").astype(jnp.bfloat16)
    pieces = [inputs] + [fetch_partner(inputs, bit_index) for bit_index in range(levels)]
    preact = jnp.dot(latent, rank_up, preferred_element_type=jnp.float32)
    for level_index in range(levels + 1):
        product = jnp.dot(
            pieces[level_index], up_blocks[level_index], preferred_element_type=jnp.float32
        )
        preact = preact + column_mask[level_index].astype(jnp.float32) * product
    hidden = jax.nn.silu(preact).astype(jnp.bfloat16)
    sigmoid_value = jax.nn.sigmoid(preact)
    slope = sigmoid_value * (1.0 + preact * (1.0 - sigmoid_value))
    grad_pre = (cotangent.astype(jnp.float32) * slope).astype(jnp.bfloat16)
    mid_part = right_transpose(grad_pre, rank_up)
    mid = lax.psum(mid_part, "wide").astype(jnp.bfloat16)
    input_acc = right_transpose(mid, rank_down)
    block_terms = []
    for level_index in range(levels + 1):
        masked = grad_pre * column_mask[level_index]
        contrib = right_transpose(masked, up_blocks[level_index])
        if level_index == 0:
            input_acc = input_acc + contrib
        else:
            input_acc = input_acc + return_partner(contrib, level_index - 1)
        level_term = gram_product(pieces[level_index], masked)
        block_terms.append(level_term)
    stacked = jnp.stack(block_terms)
    up_term = gram_product(latent, grad_pre)
    down_term = gram_product(inputs, mid)
    stacked, up_term, down_term = lax.psum((stacked, up_term, down_term), "dp")
    block_grad = (grad_scale * stacked).astype(jnp.bfloat16)
    up_grad = (grad_scale * up_term).astype(jnp.bfloat16)
    down_grad = (grad_scale * down_term).astype(jnp.bfloat16)
    input_grad = input_acc.astype(jnp.bfloat16)
    return (hidden, input_grad, block_grad, up_grad, down_grad)


TILE_ROWS = 16
MESH = pl.DeviceIdType.MESH


def fused_kernel(
    dims, x_in, cot_in, blocks_in, links, down_in, up_in,
    hidden, input_grad, block_grad, up_grad, down_grad,
    pieces, latent, grads, mid, weights, down, cot, blocks,
    part, part_send, sums, base, contrib_send, contrib_got,
    send_sem, recv_sem, local_sem, scatter_sem, sums_sem, gather_sem, chunk_sem,
):
    width, copies, levels, scale = dims
    tokens, features = x_in.shape
    rank = down_in.shape[1]
    units = up_in.shape[1]
    halves = links.shape[0]
    block_cols = units // halves
    me_w, me_d = lax.axis_index("wide"), lax.axis_index("dp")
    count = [0, 0]
    pending = []

    def load(source, target):
        copy = pltpu.make_async_copy(source, target, local_sem.at[count[0]])
        count[0] += 1
        copy.start()
        return copy

    def push(source, target, wide=None, dp=None):
        where = {"wide": me_w if wide is None else wide, "dp": me_d if dp is None else dp}
        copy = pltpu.make_async_remote_copy(
            src_ref=source, dst_ref=target,
            send_sem=send_sem.at[count[1]], recv_sem=recv_sem.at[count[1]],
            device_id=(where["dp"], where["wide"]), device_id_type=MESH,
        )
        count[1] += 1
        copy.start()
        pending.append(copy)
        return copy

    def rows(index, size=tokens):
        if isinstance(index, int):
            return pl.ds(index * size, size)
        return pl.ds(pl.multiple_of(index * size, size), size)

    get_x = load(x_in, pieces.at[0, rows(0)])
    get_down = load(down_in, down)
    get_up = load(up_in, weights.at[pl.ds(0, rank)])
    get_blocks = load(blocks_in, blocks)
    get_cot = load(cot_in, cot)

    first, owners = width // 4, width // 2
    chunk = tokens // owners

    def owns(index):
        return (index >= first) & (index < first + owners)

    barrier = pltpu.get_barrier_semaphore()
    expected = copies - 1
    for offset in range(1, width):
        meets = owns(me_w) | owns(me_w ^ offset)
        if offset & (offset - 1) == 0:
            meets = meets | (me_w >= 0)
        expected = expected + jnp.where(meets, 1, 0)

        @pl.when(meets)
        def _(offset=offset):
            pl.semaphore_signal(
                barrier, inc=1, device_id=(me_d, me_w ^ offset), device_id_type=MESH
            )
    for offset in range(1, copies):
        pl.semaphore_signal(
            barrier, inc=1, device_id=(me_d ^ offset, me_w), device_id_type=MESH
        )

    def scatter(turn, value):
        part[...] = value
        part_send[turn] = value.astype(jnp.bfloat16)

    def scatter_copy(turn, index, sender):
        return pltpu.make_async_remote_copy(
            src_ref=part_send.at[turn, rows(index, chunk)], dst_ref=sums.at[turn, sender],
            send_sem=scatter_sem.at[turn, index], recv_sem=sums_sem.at[turn, sender],
            device_id=(me_d, first + index), device_id_type=MESH,
        )

    def scatter_push(turn):
        for step in range(owners):
            index = jnp.where(me_w < width // 2, owners - 1 - step, step)

            @pl.when(first + index != me_w)
            def _(index=index):
                scatter_copy(turn, index, me_w).start()

    def gather_copy(turn, buffer, index, offset):
        chunk_rows = rows(index, chunk)
        return pltpu.make_async_remote_copy(
            src_ref=buffer.at[chunk_rows], dst_ref=buffer.at[chunk_rows],
            send_sem=gather_sem.at[turn, offset], recv_sem=chunk_sem.at[turn, index],
            device_id=(me_d, me_w ^ offset), device_id_type=MESH,
        )

    def reduce_and_gather(turn, buffer):
        @pl.when(owns(me_w))
        def _():
            own = me_w - first
            total = part[rows(own, chunk), :]
            for offset in range(1, width):
                sender = me_w ^ offset
                scatter_copy(turn, own, sender).wait_recv()
                total = total + sums[turn, sender].astype(jnp.float32)
            buffer[rows(own, chunk), :] = total.astype(jnp.bfloat16)
            for offset in range(width - 1, 0, -1):
                gather_copy(turn, buffer, own, offset).start()

    def near_chunk(step):
        return jnp.where(me_w < width // 2, step, owners - 1 - step)

    def wait_chunk(turn, buffer, index):
        @pl.when(first + index != me_w)
        def _():
            gather_copy(turn, buffer, index, 1).wait_recv()

    def finish(turn, buffer):
        for index in range(owners):
            @pl.when(first + index != me_w)
            def _(index=index):
                scatter_copy(turn, index, me_w).wait_send()

        @pl.when(owns(me_w))
        def _():
            for offset in range(1, width):
                gather_copy(turn, buffer, me_w - first, offset).wait_send()

    get_x.wait()
    get_down.wait()
    x = pieces[0, 0:tokens, :]
    scatter(0, jnp.dot(x, down[...], preferred_element_type=jnp.float32))
    pl.semaphore_wait(barrier, expected)
    scatter_push(0)
    fetched = [
        push(pieces.at[0, rows(0)], pieces.at[level, rows(0)], wide=me_w ^ (1 << (level - 1)))
        for level in range(1, levels + 1)
    ]
    across, aside = {}, {}

    def spread(name, buffer_slot):
        aside[name] = push(buffer_slot(0), buffer_slot(1), dp=me_d ^ 1)
        across[name] = push(buffer_slot(0), buffer_slot(2), dp=me_d ^ 2)

    def relay(name, buffer_slot):
        across[name].wait_recv()
        return push(buffer_slot(2), buffer_slot(3), dp=me_d ^ 1)

    def piece_slot(level):
        return lambda slot: pieces.at[level, rows(slot)]

    def latent_slot(slot):
        return latent.at[rows(slot)]

    def grads_slot(slot):
        return grads.at[rows(slot)]

    spread(("piece", 0), piece_slot(0))

    get_blocks.wait()
    for level in range(levels + 1):
        for block in range(halves):
            cols = pl.ds(block * block_cols, block_cols)
            keep = links[block, level].astype(jnp.float32).astype(jnp.bfloat16)
            weights[pl.ds(rank + level * features, features), cols] = (
                blocks[level, :, cols] * keep
            )

    reduce_and_gather(0, latent)

    get_up.wait()
    for level in range(1, levels + 1):
        fetched[level - 1].wait_recv()
        spread(("piece", level), piece_slot(level))
    own_pieces = jnp.concatenate(
        [pieces[level, 0:tokens, :] for level in range(levels + 1)], axis=1
    )
    base[...] = jnp.dot(own_pieces, weights[rank:, :], preferred_element_type=jnp.float32)
    get_cot.wait()

    for step in range(owners):
        wait_chunk(0, latent, near_chunk(step))
    spread("latent", latent_slot)
    preact = base[...] + jnp.dot(
        latent[0:tokens, :], weights[0:rank, :], preferred_element_type=jnp.float32
    )
    sig = 1.0 / (1.0 + jnp.exp(-preact))
    slope = sig * (1.0 + preact * (1.0 - sig))
    grad_pre = (cot[...].astype(jnp.float32) * slope).astype(jnp.bfloat16)
    grads[0:tokens, :] = grad_pre
    hidden[...] = (preact * sig).astype(jnp.bfloat16)

    def back(lo, hi):
        return lax.dot_general(
            grads[0:tokens, :], weights[lo:hi, :], (((1,), (1,)), ((), ())),
            preferred_element_type=jnp.float32,
        )

    scatter(1, back(0, rank))
    scatter_push(1)
    spread("grads", grads_slot)
    contrib = back(rank, rank + (levels + 1) * features)
    returned = []
    for level in range(1, levels + 1):
        contrib_send[level - 1] = contrib[:, level * features:(level + 1) * features].astype(
            jnp.bfloat16
        )
        returned.append(
            push(
                contrib_send.at[level - 1], contrib_got.at[level - 1],
                wide=me_w ^ (1 << (level - 1)),
            )
        )
    base[:, 0:features] = contrib[:, 0:features]

    relayed = [relay(("piece", level), piece_slot(level)) for level in range(levels + 1)]
    relayed.append(relay("latent", latent_slot))

    reduce_and_gather(1, mid)
    relayed.append(relay("grads", grads_slot))

    def gram(left, right):
        return lax.dot_general(
            left, right, (((0,), (0,)), ((), ())), preferred_element_type=jnp.float32
        )

    for copy in aside.values():
        copy.wait_recv()
    for copy in relayed:
        copy.wait_recv()
    up_grad[...] = (scale * gram(latent[...], grads[...])).astype(jnp.bfloat16)
    for level in range(levels + 1):
        term = scale * gram(pieces[level], grads[...])
        for block in range(halves):
            cols = slice(block * block_cols, (block + 1) * block_cols)
            keep = links[block, level].astype(jnp.float32)
            block_grad[level, :, cols] = (term[:, cols] * keep).astype(jnp.bfloat16)

    mid_spread = []
    for step in range(owners):
        index = near_chunk(step)
        wait_chunk(1, mid, index)
        for slot in range(1, copies):
            target = pl.ds(pl.multiple_of(slot * tokens + index * chunk, chunk), chunk)
            mid_spread.append(push(mid.at[rows(index, chunk)], mid.at[target], dp=me_d ^ slot))
    total = base[:, 0:features] + lax.dot_general(
        mid[0:tokens, :], down[...], (((1,), (1,)), ((), ())),
        preferred_element_type=jnp.float32,
    )
    for level in range(levels):
        returned[level].wait_recv()
        total = total + contrib_got[level].astype(jnp.float32)
    input_grad[...] = total.astype(jnp.bfloat16)
    for copy in mid_spread:
        copy.wait_recv()
    down_grad[...] = (scale * gram(pieces[0], mid[...])).astype(jnp.bfloat16)
    for copy in pending:
        copy.wait_send()
    finish(0, latent)
    finish(1, mid)


def store_kernel(*refs):
    sem = refs[-1]
    copies = [
        pltpu.make_async_copy(source, target, sem.at[i])
        for i, (source, target) in enumerate(zip(refs[:5], refs[5:10]))
    ]
    for copy in copies:
        copy.start()
    for copy in copies:
        copy.wait()


def fused(inputs, cotangent, up_blocks, block_links, rank_down, rank_up):
    width, copies = lax.axis_size("wide"), lax.axis_size("dp")
    tokens, features = inputs.shape
    level_count = up_blocks.shape[0]
    rank, units = rank_up.shape
    scale = 1.0 / math.sqrt(tokens * copies)
    levels = level_count - 1
    owners = width // 2
    chunk = tokens // owners
    remote = 2 * levels + 3 * (levels + 1) + 6 + 3 * owners
    half, full = jnp.bfloat16, jnp.float32
    shapes = (
        ((tokens, units), half), ((tokens, features), half), (up_blocks.shape, half),
        ((rank, units), half), ((features, rank), half),
    )
    anywhere = pl.BlockSpec(memory_space=pl.ANY)
    results = pl.pallas_call(
        functools.partial(fused_kernel, (width, copies, levels, scale)),
        out_shape=[pltpu.VMEM(*entry) for entry in shapes],
        in_specs=[anywhere] * 3 + [pl.BlockSpec(memory_space=pltpu.SMEM)] + [anywhere] * 2,
        out_specs=[pl.BlockSpec(memory_space=pltpu.VMEM)] * 5,
        scratch_shapes=[
            pltpu.VMEM((level_count, copies * tokens, features), half),
            pltpu.VMEM((copies * tokens, rank), half),
            pltpu.VMEM((copies * tokens, units), half),
            pltpu.VMEM((copies * tokens, rank), half),
            pltpu.VMEM((rank + level_count * features, units), half),
            pltpu.VMEM((features, rank), half),
            pltpu.VMEM((tokens, units), half),
            pltpu.VMEM(up_blocks.shape, half),
            pltpu.VMEM((tokens, rank), full),
            pltpu.VMEM((2, tokens, rank), half),
            pltpu.VMEM((2, width, chunk, rank), half),
            pltpu.VMEM((tokens, units), full),
            pltpu.VMEM((levels, tokens, features), half),
            pltpu.VMEM((levels, tokens, features), half),
            pltpu.SemaphoreType.DMA((remote,)),
            pltpu.SemaphoreType.DMA((remote,)),
            pltpu.SemaphoreType.DMA((5,)),
            pltpu.SemaphoreType.DMA((2, owners)),
            pltpu.SemaphoreType.DMA((2, width)),
            pltpu.SemaphoreType.DMA((2, width)),
            pltpu.SemaphoreType.DMA((2, owners)),
        ],
        compiler_params=pltpu.CompilerParams(collective_id=0, has_side_effects=True),
    )(inputs, cotangent, up_blocks, block_links.T, rank_down, rank_up)
    return pl.pallas_call(
        store_kernel,
        out_shape=[jax.ShapeDtypeStruct(*entry) for entry in shapes],
        in_specs=[pl.BlockSpec(memory_space=pltpu.VMEM)] * 5,
        out_specs=[pl.BlockSpec(memory_space=pltpu.HBM)] * 5,
        scratch_shapes=[pltpu.SemaphoreType.DMA((5,))],
    )(*results)


def choose(inputs, *others):
    fits = inputs.shape[0] % (TILE_ROWS * lax.axis_size("wide") // 2) == 0 and lax.axis_size("dp") == 4
    return (fused if fits else on_device)(inputs, *others)


def solution(mesh):
    in_specs = (
        P("dp", "wide"),
        P("dp", "wide"),
        P(None, None, "wide"),
        P(None, "wide"),
        P("wide", None),
        P(None, "wide"),
    )
    out_specs = (
        P("dp", "wide"),
        P("dp", "wide"),
        P(None, None, "wide"),
        P(None, "wide"),
        P("wide", None),
    )
    return jax.shard_map(
        choose, mesh=mesh, in_specs=in_specs, out_specs=out_specs, check_vma=False
    )
```

```python
import functools
import math

import jax
import jax.numpy as jnp
from jax import lax
from jax.experimental import pallas as pl
from jax.experimental.pallas import tpu as pltpu
from jax.sharding import PartitionSpec as P


def partner(shard, axis, distance):
    return lax.ppermute(shard, axis, [(i, i ^ 1 << distance) for i in range(lax.axis_size(axis))])


def fetch_partner(values, bit_index):
    return partner(values, "wide", bit_index)


def return_partner(values, bit_index):
    return partner(values, "wide", bit_index)


def gram_product(left, right):
    return lax.dot_general(
        left, right, (((0,), (0,)), ((), ())), preferred_element_type=jnp.float32
    )


def right_transpose(left, right):
    return lax.dot_general(
        left, right, (((1,), (1,)), ((), ())), preferred_element_type=jnp.float32
    )


def on_device(inputs, cotangent, up_blocks, block_links, rank_down, rank_up):
    width_count = lax.axis_size("wide")
    levels = min(6, 3 + 3 * (width_count // 64))
    tokens_all = inputs.shape[0] * lax.axis_size("dp")
    grad_scale = 1.0 / math.sqrt(tokens_all)
    block_cols = up_blocks.shape[2] // block_links.shape[1]
    column_mask = jnp.repeat(block_links, block_cols, axis=1).astype(jnp.bfloat16)
    latent_part = jnp.dot(inputs, rank_down, preferred_element_type=jnp.float32)
    latent = lax.psum(latent_part, "wide").astype(jnp.bfloat16)
    pieces = [inputs] + [fetch_partner(inputs, bit_index) for bit_index in range(levels)]
    preact = jnp.dot(latent, rank_up, preferred_element_type=jnp.float32)
    for level_index in range(levels + 1):
        product = jnp.dot(
            pieces[level_index], up_blocks[level_index], preferred_element_type=jnp.float32
        )
        preact = preact + column_mask[level_index].astype(jnp.float32) * product
    hidden = jax.nn.silu(preact).astype(jnp.bfloat16)
    sigmoid_value = jax.nn.sigmoid(preact)
    slope = sigmoid_value * (1.0 + preact * (1.0 - sigmoid_value))
    grad_pre = (cotangent.astype(jnp.float32) * slope).astype(jnp.bfloat16)
    mid_part = right_transpose(grad_pre, rank_up)
    mid = lax.psum(mid_part, "wide").astype(jnp.bfloat16)
    input_acc = right_transpose(mid, rank_down)
    block_terms = []
    for level_index in range(levels + 1):
        masked = grad_pre * column_mask[level_index]
        contrib = right_transpose(masked, up_blocks[level_index])
        if level_index == 0:
            input_acc = input_acc + contrib
        else:
            input_acc = input_acc + return_partner(contrib, level_index - 1)
        level_term = gram_product(pieces[level_index], masked)
        block_terms.append(level_term)
    stacked = jnp.stack(block_terms)
    up_term = gram_product(latent, grad_pre)
    down_term = gram_product(inputs, mid)
    stacked, up_term, down_term = lax.psum((stacked, up_term, down_term), "dp")
    block_grad = (grad_scale * stacked).astype(jnp.bfloat16)
    up_grad = (grad_scale * up_term).astype(jnp.bfloat16)
    down_grad = (grad_scale * down_term).astype(jnp.bfloat16)
    input_grad = input_acc.astype(jnp.bfloat16)
    return (hidden, input_grad, block_grad, up_grad, down_grad)


TILE_ROWS = 16
MESH = pl.DeviceIdType.MESH


def fused_kernel(
    dims, x_in, cot_in, blocks_in, links, down_in, up_in,
    hidden, input_grad, block_grad, up_grad, down_grad,
    pieces, latent, grads, mid, weights, down, cot, blocks,
    part, part_send, sums, base, contrib_send, contrib_got,
    send_sem, recv_sem, local_sem, scatter_sem, sums_sem, gather_sem, chunk_sem,
):
    width, copies, levels, scale = dims
    tokens, features = x_in.shape
    rank = down_in.shape[1]
    units = up_in.shape[1]
    halves = links.shape[0]
    block_cols = units // halves
    me_w, me_d = lax.axis_index("wide"), lax.axis_index("dp")
    count = [0, 0]
    pending = []

    def load(source, target):
        copy = pltpu.make_async_copy(source, target, local_sem.at[count[0]])
        count[0] += 1
        copy.start()
        return copy

    def push(source, target, wide=None, dp=None):
        where = {"wide": me_w if wide is None else wide, "dp": me_d if dp is None else dp}
        copy = pltpu.make_async_remote_copy(
            src_ref=source, dst_ref=target,
            send_sem=send_sem.at[count[1]], recv_sem=recv_sem.at[count[1]],
            device_id=(where["dp"], where["wide"]), device_id_type=MESH,
        )
        count[1] += 1
        copy.start()
        pending.append(copy)
        return copy

    def rows(index, size=tokens):
        if isinstance(index, int):
            return pl.ds(index * size, size)
        return pl.ds(pl.multiple_of(index * size, size), size)

    get_x = load(x_in, pieces.at[0, rows(0)])
    get_down = load(down_in, down)
    get_up = load(up_in, weights.at[pl.ds(0, rank)])
    get_blocks = load(blocks_in, blocks)
    get_cot = load(cot_in, cot)

    first, owners = width // 4, width // 2
    chunk = tokens // owners

    def owns(index):
        return (index >= first) & (index < first + owners)

    barrier = pltpu.get_barrier_semaphore()
    expected = copies - 1
    for offset in range(1, width):
        meets = owns(me_w) | owns(me_w ^ offset)
        if offset & (offset - 1) == 0:
            meets = meets | (me_w >= 0)
        expected = expected + jnp.where(meets, 1, 0)

        @pl.when(meets)
        def _(offset=offset):
            pl.semaphore_signal(
                barrier, inc=1, device_id=(me_d, me_w ^ offset), device_id_type=MESH
            )
    for offset in range(1, copies):
        pl.semaphore_signal(
            barrier, inc=1, device_id=(me_d ^ offset, me_w), device_id_type=MESH
        )

    def scatter(turn, value):
        part[...] = value
        part_send[turn] = value.astype(jnp.bfloat16)

    def scatter_copy(turn, index, sender):
        return pltpu.make_async_remote_copy(
            src_ref=part_send.at[turn, rows(index, chunk)], dst_ref=sums.at[turn, sender],
            send_sem=scatter_sem.at[turn, index], recv_sem=sums_sem.at[turn, sender],
            device_id=(me_d, first + index), device_id_type=MESH,
        )

    def scatter_push(turn):
        for step in range(owners):
            index = jnp.where(me_w < width // 2, owners - 1 - step, step)

            @pl.when(first + index != me_w)
            def _(index=index):
                scatter_copy(turn, index, me_w).start()

    def gather_copy(turn, buffer, index, offset):
        chunk_rows = rows(index, chunk)
        return pltpu.make_async_remote_copy(
            src_ref=buffer.at[chunk_rows], dst_ref=buffer.at[chunk_rows],
            send_sem=gather_sem.at[turn, offset], recv_sem=chunk_sem.at[turn, index],
            device_id=(me_d, me_w ^ offset), device_id_type=MESH,
        )

    def reduce_and_gather(turn, buffer):
        @pl.when(owns(me_w))
        def _():
            own = me_w - first
            total = part[rows(own, chunk), :]
            for offset in range(1, width):
                sender = me_w ^ offset
                scatter_copy(turn, own, sender).wait_recv()
                total = total + sums[turn, sender].astype(jnp.float32)
            buffer[rows(own, chunk), :] = total.astype(jnp.bfloat16)
            for offset in range(width - 1, 0, -1):
                gather_copy(turn, buffer, own, offset).start()

    def near_chunk(step):
        return jnp.where(me_w < width // 2, step, owners - 1 - step)

    def wait_chunk(turn, buffer, index):
        @pl.when(first + index != me_w)
        def _():
            gather_copy(turn, buffer, index, 1).wait_recv()

    def finish(turn, buffer):
        for index in range(owners):
            @pl.when(first + index != me_w)
            def _(index=index):
                scatter_copy(turn, index, me_w).wait_send()

        @pl.when(owns(me_w))
        def _():
            for offset in range(1, width):
                gather_copy(turn, buffer, me_w - first, offset).wait_send()

    get_x.wait()
    get_down.wait()
    x = pieces[0, 0:tokens, :]
    scatter(0, jnp.dot(x, down[...], preferred_element_type=jnp.float32))
    pl.semaphore_wait(barrier, expected)
    scatter_push(0)
    fetched = [
        push(pieces.at[0, rows(0)], pieces.at[level, rows(0)], wide=me_w ^ (1 << (level - 1)))
        for level in range(1, levels + 1)
    ]
    across, aside = {}, {}

    def spread(name, buffer_slot):
        aside[name] = push(buffer_slot(0), buffer_slot(1), dp=me_d ^ 1)
        across[name] = push(buffer_slot(0), buffer_slot(2), dp=me_d ^ 2)

    def relay(name, buffer_slot):
        across[name].wait_recv()
        return push(buffer_slot(2), buffer_slot(3), dp=me_d ^ 1)

    def piece_slot(level):
        return lambda slot: pieces.at[level, rows(slot)]

    def latent_slot(slot):
        return latent.at[rows(slot)]

    def grads_slot(slot):
        return grads.at[rows(slot)]

    spread(("piece", 0), piece_slot(0))

    get_blocks.wait()
    for level in range(levels + 1):
        for block in range(halves):
            cols = pl.ds(block * block_cols, block_cols)
            keep = links[block, level].astype(jnp.float32).astype(jnp.bfloat16)
            weights[pl.ds(rank + level * features, features), cols] = (
                blocks[level, :, cols] * keep
            )

    reduce_and_gather(0, latent)

    get_up.wait()
    for level in range(1, levels + 1):
        fetched[level - 1].wait_recv()
        spread(("piece", level), piece_slot(level))
    own_pieces = jnp.concatenate(
        [pieces[level, 0:tokens, :] for level in range(levels + 1)], axis=1
    )
    base[...] = jnp.dot(own_pieces, weights[rank:, :], preferred_element_type=jnp.float32)
    get_cot.wait()

    for step in range(owners):
        wait_chunk(0, latent, near_chunk(step))
    spread("latent", latent_slot)
    preact = base[...] + jnp.dot(
        latent[0:tokens, :], weights[0:rank, :], preferred_element_type=jnp.float32
    )
    sig = 1.0 / (1.0 + jnp.exp(-preact))
    slope = sig * (1.0 + preact * (1.0 - sig))
    grad_pre = (cot[...].astype(jnp.float32) * slope).astype(jnp.bfloat16)
    grads[0:tokens, :] = grad_pre
    hidden[...] = (preact * sig).astype(jnp.bfloat16)

    def back(lo, hi):
        return lax.dot_general(
            grads[0:tokens, :], weights[lo:hi, :], (((1,), (1,)), ((), ())),
            preferred_element_type=jnp.float32,
        )

    scatter(1, back(0, rank))
    scatter_push(1)
    spread("grads", grads_slot)
    contrib = back(rank, rank + (levels + 1) * features)
    returned = []
    for level in range(1, levels + 1):
        contrib_send[level - 1] = contrib[:, level * features:(level + 1) * features].astype(
            jnp.bfloat16
        )
        returned.append(
            push(
                contrib_send.at[level - 1], contrib_got.at[level - 1],
                wide=me_w ^ (1 << (level - 1)),
            )
        )
    base[:, 0:features] = contrib[:, 0:features]

    relayed = [relay(("piece", level), piece_slot(level)) for level in range(levels + 1)]
    relayed.append(relay("latent", latent_slot))

    reduce_and_gather(1, mid)
    relayed.append(relay("grads", grads_slot))

    def gram(left, right):
        return lax.dot_general(
            left, right, (((0,), (0,)), ((), ())), preferred_element_type=jnp.float32
        )

    for copy in aside.values():
        copy.wait_recv()
    for copy in relayed:
        copy.wait_recv()
    up_grad[...] = (scale * gram(latent[...], grads[...])).astype(jnp.bfloat16)
    for level in range(levels + 1):
        term = scale * gram(pieces[level], grads[...])
        for block in range(halves):
            cols = slice(block * block_cols, (block + 1) * block_cols)
            keep = links[block, level].astype(jnp.float32)
            block_grad[level, :, cols] = (term[:, cols] * keep).astype(jnp.bfloat16)

    mid_spread = []
    for step in range(owners):
        index = near_chunk(step)
        wait_chunk(1, mid, index)
        for slot in range(1, copies):
            target = pl.ds(pl.multiple_of(slot * tokens + index * chunk, chunk), chunk)
            mid_spread.append(push(mid.at[rows(index, chunk)], mid.at[target], dp=me_d ^ slot))
    total = base[:, 0:features] + lax.dot_general(
        mid[0:tokens, :], down[...], (((1,), (1,)), ((), ())),
        preferred_element_type=jnp.float32,
    )
    for level in range(levels):
        returned[level].wait_recv()
        total = total + contrib_got[level].astype(jnp.float32)
    input_grad[...] = total.astype(jnp.bfloat16)
    for copy in mid_spread:
        copy.wait_recv()
    down_grad[...] = (scale * gram(pieces[0], mid[...])).astype(jnp.bfloat16)
    for copy in pending:
        copy.wait_send()
    finish(0, latent)
    finish(1, mid)


def store_kernel(*refs):
    sem = refs[-1]
    copies = [
        pltpu.make_async_copy(source, target, sem.at[i])
        for i, (source, target) in enumerate(zip(refs[:5], refs[5:10]))
    ]
    for copy in copies:
        copy.start()
    for copy in copies:
        copy.wait()


def fused(inputs, cotangent, up_blocks, block_links, rank_down, rank_up):
    width, copies = lax.axis_size("wide"), lax.axis_size("dp")
    tokens, features = inputs.shape
    level_count = up_blocks.shape[0]
    rank, units = rank_up.shape
    scale = 1.0 / math.sqrt(tokens * copies)
    levels = level_count - 1
    owners = width // 2
    chunk = tokens // owners
    remote = 2 * levels + 3 * (levels + 1) + 6 + 3 * owners
    half, full = jnp.bfloat16, jnp.float32
    shapes = (
        ((tokens, units), half), ((tokens, features), half), (up_blocks.shape, half),
        ((rank, units), half), ((features, rank), half),
    )
    anywhere = pl.BlockSpec(memory_space=pl.ANY)
    results = pl.pallas_call(
        functools.partial(fused_kernel, (width, copies, levels, scale)),
        out_shape=[pltpu.VMEM(*entry) for entry in shapes],
        in_specs=[anywhere] * 3 + [pl.BlockSpec(memory_space=pltpu.SMEM)] + [anywhere] * 2,
        out_specs=[pl.BlockSpec(memory_space=pltpu.VMEM)] * 5,
        scratch_shapes=[
            pltpu.VMEM((level_count, copies * tokens, features), half),
            pltpu.VMEM((copies * tokens, rank), half),
            pltpu.VMEM((copies * tokens, units), half),
            pltpu.VMEM((copies * tokens, rank), half),
            pltpu.VMEM((rank + level_count * features, units), half),
            pltpu.VMEM((features, rank), half),
            pltpu.VMEM((tokens, units), half),
            pltpu.VMEM(up_blocks.shape, half),
            pltpu.VMEM((tokens, rank), full),
            pltpu.VMEM((2, tokens, rank), half),
            pltpu.VMEM((2, width, chunk, rank), half),
            pltpu.VMEM((tokens, units), full),
            pltpu.VMEM((levels, tokens, features), half),
            pltpu.VMEM((levels, tokens, features), half),
            pltpu.SemaphoreType.DMA((remote,)),
            pltpu.SemaphoreType.DMA((remote,)),
            pltpu.SemaphoreType.DMA((5,)),
            pltpu.SemaphoreType.DMA((2, owners)),
            pltpu.SemaphoreType.DMA((2, width)),
            pltpu.SemaphoreType.DMA((2, width)),
            pltpu.SemaphoreType.DMA((2, owners)),
        ],
        compiler_params=pltpu.CompilerParams(collective_id=0, has_side_effects=True),
    )(inputs, cotangent, up_blocks, block_links.T, rank_down, rank_up)
    return pl.pallas_call(
        store_kernel,
        out_shape=[jax.ShapeDtypeStruct(*entry) for entry in shapes],
        in_specs=[pl.BlockSpec(memory_space=pltpu.VMEM)] * 5,
        out_specs=[pl.BlockSpec(memory_space=pltpu.HBM)] * 5,
        scratch_shapes=[pltpu.SemaphoreType.DMA((5,))],
    )(*(pltpu.with_memory_space_constraint(result, pltpu.VMEM) for result in results))


def choose(inputs, *others):
    fits = inputs.shape[0] % (TILE_ROWS * lax.axis_size("wide") // 2) == 0 and lax.axis_size("dp") == 4
    return (fused if fits else on_device)(inputs, *others)


def solution(mesh):
    in_specs = (
        P("dp", "wide"),
        P("dp", "wide"),
        P(None, None, "wide"),
        P(None, "wide"),
        P("wide", None),
        P(None, "wide"),
    )
    out_specs = (
        P("dp", "wide"),
        P("dp", "wide"),
        P(None, None, "wide"),
        P(None, "wide"),
        P("wide", None),
    )
    return jax.shard_map(
        choose, mesh=mesh, in_specs=in_specs, out_specs=out_specs, check_vma=False
    )
```

```python
import functools
import math

import jax
import jax.numpy as jnp
from jax import lax
from jax.experimental import pallas as pl
from jax.experimental.pallas import tpu as pltpu
from jax.sharding import PartitionSpec as P


def partner(shard, axis, distance):
    return lax.ppermute(shard, axis, [(i, i ^ 1 << distance) for i in range(lax.axis_size(axis))])


def fetch_partner(values, bit_index):
    return partner(values, "wide", bit_index)


def return_partner(values, bit_index):
    return partner(values, "wide", bit_index)


def gram_product(left, right):
    return lax.dot_general(
        left, right, (((0,), (0,)), ((), ())), preferred_element_type=jnp.float32
    )


def right_transpose(left, right):
    return lax.dot_general(
        left, right, (((1,), (1,)), ((), ())), preferred_element_type=jnp.float32
    )


def on_device(inputs, cotangent, up_blocks, block_links, rank_down, rank_up):
    width_count = lax.axis_size("wide")
    levels = min(6, 3 + 3 * (width_count // 64))
    tokens_all = inputs.shape[0] * lax.axis_size("dp")
    grad_scale = 1.0 / math.sqrt(tokens_all)
    block_cols = up_blocks.shape[2] // block_links.shape[1]
    column_mask = jnp.repeat(block_links, block_cols, axis=1).astype(jnp.bfloat16)
    latent_part = jnp.dot(inputs, rank_down, preferred_element_type=jnp.float32)
    latent = lax.psum(latent_part, "wide").astype(jnp.bfloat16)
    pieces = [inputs] + [fetch_partner(inputs, bit_index) for bit_index in range(levels)]
    preact = jnp.dot(latent, rank_up, preferred_element_type=jnp.float32)
    for level_index in range(levels + 1):
        product = jnp.dot(
            pieces[level_index], up_blocks[level_index], preferred_element_type=jnp.float32
        )
        preact = preact + column_mask[level_index].astype(jnp.float32) * product
    hidden = jax.nn.silu(preact).astype(jnp.bfloat16)
    sigmoid_value = jax.nn.sigmoid(preact)
    slope = sigmoid_value * (1.0 + preact * (1.0 - sigmoid_value))
    grad_pre = (cotangent.astype(jnp.float32) * slope).astype(jnp.bfloat16)
    mid_part = right_transpose(grad_pre, rank_up)
    mid = lax.psum(mid_part, "wide").astype(jnp.bfloat16)
    input_acc = right_transpose(mid, rank_down)
    block_terms = []
    for level_index in range(levels + 1):
        masked = grad_pre * column_mask[level_index]
        contrib = right_transpose(masked, up_blocks[level_index])
        if level_index == 0:
            input_acc = input_acc + contrib
        else:
            input_acc = input_acc + return_partner(contrib, level_index - 1)
        level_term = gram_product(pieces[level_index], masked)
        block_terms.append(level_term)
    stacked = jnp.stack(block_terms)
    up_term = gram_product(latent, grad_pre)
    down_term = gram_product(inputs, mid)
    stacked, up_term, down_term = lax.psum((stacked, up_term, down_term), "dp")
    block_grad = (grad_scale * stacked).astype(jnp.bfloat16)
    up_grad = (grad_scale * up_term).astype(jnp.bfloat16)
    down_grad = (grad_scale * down_term).astype(jnp.bfloat16)
    input_grad = input_acc.astype(jnp.bfloat16)
    return (hidden, input_grad, block_grad, up_grad, down_grad)


TILE_ROWS = 16
MESH = pl.DeviceIdType.MESH


def fused_kernel(
    dims, x_in, cot_in, blocks_in, links, down_in, up_in,
    hidden, input_grad, block_grad, up_grad, down_grad,
    pieces, latent, grads, mid, weights, down, cot, blocks,
    part, part_send, sums, base, contrib_send, contrib_got,
    send_sem, recv_sem, local_sem, scatter_sem, sums_sem, gather_sem, chunk_sem,
):
    width, copies, levels, scale = dims
    tokens, features = x_in.shape
    rank = down_in.shape[1]
    units = up_in.shape[1]
    halves = links.shape[0]
    block_cols = units // halves
    me_w, me_d = lax.axis_index("wide"), lax.axis_index("dp")
    count = [0, 0]
    pending = []

    def load(source, target):
        copy = pltpu.make_async_copy(source, target, local_sem.at[count[0]])
        count[0] += 1
        copy.start()
        return copy

    def push(source, target, wide=None, dp=None):
        where = {"wide": me_w if wide is None else wide, "dp": me_d if dp is None else dp}
        copy = pltpu.make_async_remote_copy(
            src_ref=source, dst_ref=target,
            send_sem=send_sem.at[count[1]], recv_sem=recv_sem.at[count[1]],
            device_id=(where["dp"], where["wide"]), device_id_type=MESH,
        )
        count[1] += 1
        copy.start()
        pending.append(copy)
        return copy

    def rows(index, size=tokens):
        if isinstance(index, int):
            return pl.ds(index * size, size)
        return pl.ds(pl.multiple_of(index * size, size), size)

    first, owners = width // 4, width // 2
    chunk = tokens // owners

    def owns(index):
        return (index >= first) & (index < first + owners)

    barrier = pltpu.get_barrier_semaphore()
    expected = copies - 1
    for offset in range(1, width):
        meets = owns(me_w) | owns(me_w ^ offset)
        if offset & (offset - 1) == 0:
            meets = meets | (me_w >= 0)
        expected = expected + jnp.where(meets, 1, 0)

        @pl.when(meets)
        def _(offset=offset):
            pl.semaphore_signal(
                barrier, inc=1, device_id=(me_d, me_w ^ offset), device_id_type=MESH
            )
    for offset in range(1, copies):
        pl.semaphore_signal(
            barrier, inc=1, device_id=(me_d ^ offset, me_w), device_id_type=MESH
        )

    get_x = load(x_in, pieces.at[0, rows(0)])
    get_down = load(down_in, down)
    get_up = load(up_in, weights.at[pl.ds(0, rank)])
    get_blocks = load(blocks_in, blocks)
    get_cot = load(cot_in, cot)

    def scatter(turn, value):
        part[...] = value
        part_send[turn] = value.astype(jnp.bfloat16)

    def scatter_copy(turn, index, sender):
        return pltpu.make_async_remote_copy(
            src_ref=part_send.at[turn, rows(index, chunk)], dst_ref=sums.at[turn, sender],
            send_sem=scatter_sem.at[turn, index], recv_sem=sums_sem.at[turn, sender],
            device_id=(me_d, first + index), device_id_type=MESH,
        )

    def scatter_push(turn):
        for step in range(owners):
            index = jnp.where(me_w < width // 2, owners - 1 - step, step)

            @pl.when(first + index != me_w)
            def _(index=index):
                scatter_copy(turn, index, me_w).start()

    def gather_copy(turn, buffer, index, offset):
        chunk_rows = rows(index, chunk)
        return pltpu.make_async_remote_copy(
            src_ref=buffer.at[chunk_rows], dst_ref=buffer.at[chunk_rows],
            send_sem=gather_sem.at[turn, offset], recv_sem=chunk_sem.at[turn, index],
            device_id=(me_d, me_w ^ offset), device_id_type=MESH,
        )

    def reach(offset):
        outer, inner = divmod(offset, width // 4)
        return (outer == 2, outer == 3, outer, inner)

    def reduce_and_gather(turn, buffer):
        @pl.when(owns(me_w))
        def _():
            own = me_w - first
            total = part[rows(own, chunk), :]
            for offset in range(1, width):
                sender = me_w ^ offset
                scatter_copy(turn, own, sender).wait_recv()
                total = total + sums[turn, sender].astype(jnp.float32)
            buffer[rows(own, chunk), :] = total.astype(jnp.bfloat16)
            for offset in sorted(range(1, width), key=reach, reverse=True):
                gather_copy(turn, buffer, own, offset).start()

    def near_chunk(step):
        return jnp.where(me_w < width // 2, step, owners - 1 - step)

    def wait_chunk(turn, buffer, index):
        @pl.when(first + index != me_w)
        def _():
            gather_copy(turn, buffer, index, 1).wait_recv()

    def finish(turn, buffer):
        for index in range(owners):
            @pl.when(first + index != me_w)
            def _(index=index):
                scatter_copy(turn, index, me_w).wait_send()

        @pl.when(owns(me_w))
        def _():
            for offset in range(1, width):
                gather_copy(turn, buffer, me_w - first, offset).wait_send()

    get_x.wait()
    get_down.wait()
    x = pieces[0, 0:tokens, :]
    scatter(0, jnp.dot(x, down[...], preferred_element_type=jnp.float32))
    pl.semaphore_wait(barrier, expected)
    scatter_push(0)
    fetched = [
        push(pieces.at[0, rows(0)], pieces.at[level, rows(0)], wide=me_w ^ (1 << (level - 1)))
        for level in range(1, levels + 1)
    ]
    across, aside = {}, {}

    def spread(name, buffer_slot):
        aside[name] = push(buffer_slot(0), buffer_slot(1), dp=me_d ^ 1)
        across[name] = push(buffer_slot(0), buffer_slot(2), dp=me_d ^ 2)

    def relay(name, buffer_slot):
        across[name].wait_recv()
        return push(buffer_slot(2), buffer_slot(3), dp=me_d ^ 1)

    def piece_slot(level):
        return lambda slot: pieces.at[level, rows(slot)]

    def latent_slot(slot):
        return latent.at[rows(slot)]

    def grads_slot(slot):
        return grads.at[rows(slot)]

    spread(("piece", 0), piece_slot(0))

    get_blocks.wait()
    for level in range(levels + 1):
        for block in range(halves):
            cols = pl.ds(block * block_cols, block_cols)
            keep = links[block, level].astype(jnp.float32).astype(jnp.bfloat16)
            weights[pl.ds(rank + level * features, features), cols] = (
                blocks[level, :, cols] * keep
            )

    reduce_and_gather(0, latent)

    get_up.wait()
    for level in range(1, levels + 1):
        fetched[level - 1].wait_recv()
        spread(("piece", level), piece_slot(level))
    own_pieces = jnp.concatenate(
        [pieces[level, 0:tokens, :] for level in range(levels + 1)], axis=1
    )
    base[...] = jnp.dot(own_pieces, weights[rank:, :], preferred_element_type=jnp.float32)
    get_cot.wait()

    for step in range(owners):
        wait_chunk(0, latent, near_chunk(step))
    spread("latent", latent_slot)
    preact = base[...] + jnp.dot(
        latent[0:tokens, :], weights[0:rank, :], preferred_element_type=jnp.float32
    )
    sig = 1.0 / (1.0 + jnp.exp(-preact))
    slope = sig * (1.0 + preact * (1.0 - sig))
    grad_pre = (cot[...].astype(jnp.float32) * slope).astype(jnp.bfloat16)
    grads[0:tokens, :] = grad_pre
    hidden[...] = (preact * sig).astype(jnp.bfloat16)

    def back(lo, hi):
        return lax.dot_general(
            grads[0:tokens, :], weights[lo:hi, :], (((1,), (1,)), ((), ())),
            preferred_element_type=jnp.float32,
        )

    scatter(1, back(0, rank))
    scatter_push(1)
    spread("grads", grads_slot)
    contrib = back(rank, rank + (levels + 1) * features)
    for level in range(1, levels + 1):
        contrib_send[level - 1] = contrib[:, level * features:(level + 1) * features].astype(
            jnp.bfloat16
        )
    base[:, 0:features] = contrib[:, 0:features]

    relayed = [relay(("piece", level), piece_slot(level)) for level in range(levels + 1)]
    relayed.append(relay("latent", latent_slot))

    reduce_and_gather(1, mid)
    relayed.append(relay("grads", grads_slot))

    mid_spread = []

    def spread_chunk(step):
        index = near_chunk(step)
        wait_chunk(1, mid, index)
        for slot in range(1, copies):
            target = pl.ds(pl.multiple_of(slot * tokens + index * chunk, chunk), chunk)
            mid_spread.append(push(mid.at[rows(index, chunk)], mid.at[target], dp=me_d ^ slot))

    for step in range(owners // 2):
        spread_chunk(step)
    returned = [
        push(
            contrib_send.at[level - 1], contrib_got.at[level - 1], wide=me_w ^ (1 << (level - 1))
        )
        for level in range(1, levels + 1)
    ]

    def gram(left, right):
        return lax.dot_general(
            left, right, (((0,), (0,)), ((), ())), preferred_element_type=jnp.float32
        )

    for copy in aside.values():
        copy.wait_recv()
    for copy in relayed:
        copy.wait_recv()
    up_grad[...] = (scale * gram(latent[...], grads[...])).astype(jnp.bfloat16)
    for level in range(levels + 1):
        term = scale * gram(pieces[level], grads[...])
        for block in range(halves):
            cols = slice(block * block_cols, (block + 1) * block_cols)
            keep = links[block, level].astype(jnp.float32)
            block_grad[level, :, cols] = (term[:, cols] * keep).astype(jnp.bfloat16)

    for step in range(owners // 2, owners):
        spread_chunk(step)
    total = base[:, 0:features] + lax.dot_general(
        mid[0:tokens, :], down[...], (((1,), (1,)), ((), ())),
        preferred_element_type=jnp.float32,
    )
    for level in range(levels):
        returned[level].wait_recv()
        total = total + contrib_got[level].astype(jnp.float32)
    input_grad[...] = total.astype(jnp.bfloat16)
    for copy in mid_spread:
        copy.wait_recv()
    down_grad[...] = (scale * gram(pieces[0], mid[...])).astype(jnp.bfloat16)
    for copy in pending:
        copy.wait_send()
    finish(0, latent)
    finish(1, mid)


def store_kernel(*refs):
    sem = refs[-1]
    copies = [
        pltpu.make_async_copy(source, target, sem.at[i])
        for i, (source, target) in enumerate(zip(refs[:5], refs[5:10]))
    ]
    for copy in copies:
        copy.start()
    for copy in copies:
        copy.wait()


def fused(inputs, cotangent, up_blocks, block_links, rank_down, rank_up):
    width, copies = lax.axis_size("wide"), lax.axis_size("dp")
    tokens, features = inputs.shape
    level_count = up_blocks.shape[0]
    rank, units = rank_up.shape
    scale = 1.0 / math.sqrt(tokens * copies)
    levels = level_count - 1
    owners = width // 2
    chunk = tokens // owners
    remote = 2 * levels + 3 * (levels + 1) + 6 + 3 * owners
    half, full = jnp.bfloat16, jnp.float32
    shapes = (
        ((tokens, units), half), ((tokens, features), half), (up_blocks.shape, half),
        ((rank, units), half), ((features, rank), half),
    )
    anywhere = pl.BlockSpec(memory_space=pl.ANY)
    results = pl.pallas_call(
        functools.partial(fused_kernel, (width, copies, levels, scale)),
        out_shape=[pltpu.VMEM(*entry) for entry in shapes],
        in_specs=[anywhere] * 3 + [pl.BlockSpec(memory_space=pltpu.SMEM)] + [anywhere] * 2,
        out_specs=[pl.BlockSpec(memory_space=pltpu.VMEM)] * 5,
        scratch_shapes=[
            pltpu.VMEM((level_count, copies * tokens, features), half),
            pltpu.VMEM((copies * tokens, rank), half),
            pltpu.VMEM((copies * tokens, units), half),
            pltpu.VMEM((copies * tokens, rank), half),
            pltpu.VMEM((rank + level_count * features, units), half),
            pltpu.VMEM((features, rank), half),
            pltpu.VMEM((tokens, units), half),
            pltpu.VMEM(up_blocks.shape, half),
            pltpu.VMEM((tokens, rank), full),
            pltpu.VMEM((2, tokens, rank), half),
            pltpu.VMEM((2, width, chunk, rank), half),
            pltpu.VMEM((tokens, units), full),
            pltpu.VMEM((levels, tokens, features), half),
            pltpu.VMEM((levels, tokens, features), half),
            pltpu.SemaphoreType.DMA((remote,)),
            pltpu.SemaphoreType.DMA((remote,)),
            pltpu.SemaphoreType.DMA((5,)),
            pltpu.SemaphoreType.DMA((2, owners)),
            pltpu.SemaphoreType.DMA((2, width)),
            pltpu.SemaphoreType.DMA((2, width)),
            pltpu.SemaphoreType.DMA((2, owners)),
        ],
        compiler_params=pltpu.CompilerParams(collective_id=0, has_side_effects=True),
    )(inputs, cotangent, up_blocks, block_links.T, rank_down, rank_up)
    return pl.pallas_call(
        store_kernel,
        out_shape=[jax.ShapeDtypeStruct(*entry) for entry in shapes],
        in_specs=[pl.BlockSpec(memory_space=pltpu.VMEM)] * 5,
        out_specs=[pl.BlockSpec(memory_space=pltpu.HBM)] * 5,
        scratch_shapes=[pltpu.SemaphoreType.DMA((5,))],
    )(*(pltpu.with_memory_space_constraint(result, pltpu.VMEM) for result in results))


def choose(inputs, *others):
    fits = inputs.shape[0] % (TILE_ROWS * lax.axis_size("wide") // 2) == 0 and lax.axis_size("dp") == 4
    return (fused if fits else on_device)(inputs, *others)


def solution(mesh):
    in_specs = (
        P("dp", "wide"),
        P("dp", "wide"),
        P(None, None, "wide"),
        P(None, "wide"),
        P("wide", None),
        P(None, "wide"),
    )
    out_specs = (
        P("dp", "wide"),
        P("dp", "wide"),
        P(None, None, "wide"),
        P(None, "wide"),
        P("wide", None),
    )
    return jax.shard_map(
        choose, mesh=mesh, in_specs=in_specs, out_specs=out_specs, check_vma=False
    )
```

```python
import functools
import math

import jax
import jax.numpy as jnp
from jax import lax
from jax.experimental import pallas as pl
from jax.experimental.pallas import tpu as pltpu
from jax.sharding import PartitionSpec as P


def partner(shard, axis, distance):
    return lax.ppermute(shard, axis, [(i, i ^ 1 << distance) for i in range(lax.axis_size(axis))])


def fetch_partner(values, bit_index):
    return partner(values, "wide", bit_index)


def return_partner(values, bit_index):
    return partner(values, "wide", bit_index)


def gram_product(left, right):
    return lax.dot_general(
        left, right, (((0,), (0,)), ((), ())), preferred_element_type=jnp.float32
    )


def right_transpose(left, right):
    return lax.dot_general(
        left, right, (((1,), (1,)), ((), ())), preferred_element_type=jnp.float32
    )


def on_device(inputs, cotangent, up_blocks, block_links, rank_down, rank_up):
    width_count = lax.axis_size("wide")
    levels = min(6, 3 + 3 * (width_count // 64))
    tokens_all = inputs.shape[0] * lax.axis_size("dp")
    grad_scale = 1.0 / math.sqrt(tokens_all)
    block_cols = up_blocks.shape[2] // block_links.shape[1]
    column_mask = jnp.repeat(block_links, block_cols, axis=1).astype(jnp.bfloat16)
    latent_part = jnp.dot(inputs, rank_down, preferred_element_type=jnp.float32)
    latent = lax.psum(latent_part, "wide").astype(jnp.bfloat16)
    pieces = [inputs] + [fetch_partner(inputs, bit_index) for bit_index in range(levels)]
    preact = jnp.dot(latent, rank_up, preferred_element_type=jnp.float32)
    for level_index in range(levels + 1):
        product = jnp.dot(
            pieces[level_index], up_blocks[level_index], preferred_element_type=jnp.float32
        )
        preact = preact + column_mask[level_index].astype(jnp.float32) * product
    hidden = jax.nn.silu(preact).astype(jnp.bfloat16)
    sigmoid_value = jax.nn.sigmoid(preact)
    slope = sigmoid_value * (1.0 + preact * (1.0 - sigmoid_value))
    grad_pre = (cotangent.astype(jnp.float32) * slope).astype(jnp.bfloat16)
    mid_part = right_transpose(grad_pre, rank_up)
    mid = lax.psum(mid_part, "wide").astype(jnp.bfloat16)
    input_acc = right_transpose(mid, rank_down)
    block_terms = []
    for level_index in range(levels + 1):
        masked = grad_pre * column_mask[level_index]
        contrib = right_transpose(masked, up_blocks[level_index])
        if level_index == 0:
            input_acc = input_acc + contrib
        else:
            input_acc = input_acc + return_partner(contrib, level_index - 1)
        level_term = gram_product(pieces[level_index], masked)
        block_terms.append(level_term)
    stacked = jnp.stack(block_terms)
    up_term = gram_product(latent, grad_pre)
    down_term = gram_product(inputs, mid)
    stacked, up_term, down_term = lax.psum((stacked, up_term, down_term), "dp")
    block_grad = (grad_scale * stacked).astype(jnp.bfloat16)
    up_grad = (grad_scale * up_term).astype(jnp.bfloat16)
    down_grad = (grad_scale * down_term).astype(jnp.bfloat16)
    input_grad = input_acc.astype(jnp.bfloat16)
    return (hidden, input_grad, block_grad, up_grad, down_grad)


TILE_ROWS = 16
MESH = pl.DeviceIdType.MESH


def fused_kernel(
    dims, x_in, cot_in, blocks_in, links, down_in, up_in,
    hidden, input_grad, block_grad, up_grad, down_grad,
    pieces, latent, grads, mid, weights, down, cot, blocks,
    part, part_send, sums, base, contrib_send, contrib_got,
    send_sem, recv_sem, local_sem, scatter_sem, sums_sem, gather_sem, chunk_sem,
):
    width, copies, levels, scale = dims
    tokens, features = x_in.shape
    rank = down_in.shape[1]
    units = up_in.shape[1]
    halves = links.shape[0]
    block_cols = units // halves
    me_w, me_d = lax.axis_index("wide"), lax.axis_index("dp")
    count = [0, 0]
    pending = []

    def load(source, target):
        copy = pltpu.make_async_copy(source, target, local_sem.at[count[0]])
        count[0] += 1
        copy.start()
        return copy

    def push(source, target, wide=None, dp=None):
        where = {"wide": me_w if wide is None else wide, "dp": me_d if dp is None else dp}
        copy = pltpu.make_async_remote_copy(
            src_ref=source, dst_ref=target,
            send_sem=send_sem.at[count[1]], recv_sem=recv_sem.at[count[1]],
            device_id=(where["dp"], where["wide"]), device_id_type=MESH,
        )
        count[1] += 1
        copy.start()
        pending.append(copy)
        return copy

    def rows(index, size=tokens):
        if isinstance(index, int):
            return pl.ds(index * size, size)
        return pl.ds(pl.multiple_of(index * size, size), size)

    first, owners = width // 4, width // 2
    chunk = tokens // owners

    def owns(index):
        return (index >= first) & (index < first + owners)

    barrier = pltpu.get_barrier_semaphore()
    expected = copies - 1
    for offset in range(1, width):
        meets = owns(me_w) | owns(me_w ^ offset)
        if offset & (offset - 1) == 0:
            meets = meets | (me_w >= 0)
        expected = expected + jnp.where(meets, 1, 0)

        @pl.when(meets)
        def _(offset=offset):
            pl.semaphore_signal(
                barrier, inc=1, device_id=(me_d, me_w ^ offset), device_id_type=MESH
            )
    for offset in range(1, copies):
        pl.semaphore_signal(
            barrier, inc=1, device_id=(me_d ^ offset, me_w), device_id_type=MESH
        )

    get_x = load(x_in, pieces.at[0, rows(0)])
    get_down = load(down_in, down)
    get_up = load(up_in, weights.at[pl.ds(0, rank)])
    get_blocks = load(blocks_in, blocks)
    get_cot = load(cot_in, cot)

    def scatter(turn, value):
        part[...] = value
        part_send[turn] = value.astype(jnp.bfloat16)

    def scatter_copy(turn, index, sender):
        return pltpu.make_async_remote_copy(
            src_ref=part_send.at[turn, rows(index, chunk)], dst_ref=sums.at[turn, sender],
            send_sem=scatter_sem.at[turn, index], recv_sem=sums_sem.at[turn, sender],
            device_id=(me_d, first + index), device_id_type=MESH,
        )

    def scatter_start(turn, index):
        @pl.when(first + index != me_w)
        def _():
            scatter_copy(turn, index, me_w).start()

    def scatter_push(turn):
        for step in range(owners):
            index = jnp.where(me_w < width // 2, owners - 1 - step, step)

            scatter_start(turn, index)

    def gather_copy(turn, buffer, index, offset):
        chunk_rows = rows(index, chunk)
        return pltpu.make_async_remote_copy(
            src_ref=buffer.at[chunk_rows], dst_ref=buffer.at[chunk_rows],
            send_sem=gather_sem.at[turn, offset], recv_sem=chunk_sem.at[turn, index],
            device_id=(me_d, me_w ^ offset), device_id_type=MESH,
        )

    def reach(offset):
        outer, inner = divmod(offset, width // 4)
        return (outer == 2, outer == 3, outer, inner)

    def reduce_and_gather(turn, buffer):
        @pl.when(owns(me_w))
        def _():
            own = me_w - first
            total = part[rows(own, chunk), :]
            for offset in range(1, width):
                sender = me_w ^ offset
                scatter_copy(turn, own, sender).wait_recv()
                total = total + sums[turn, sender].astype(jnp.float32)
            buffer[rows(own, chunk), :] = total.astype(jnp.bfloat16)
            for offset in sorted(range(1, width), key=reach, reverse=True):
                gather_copy(turn, buffer, own, offset).start()

    def near_chunk(step):
        return jnp.where(me_w < width // 2, step, owners - 1 - step)

    def wait_chunk(turn, buffer, index):
        @pl.when(first + index != me_w)
        def _():
            gather_copy(turn, buffer, index, 1).wait_recv()

    def finish(turn, buffer):
        for index in range(owners):
            @pl.when(first + index != me_w)
            def _(index=index):
                scatter_copy(turn, index, me_w).wait_send()

        @pl.when(owns(me_w))
        def _():
            for offset in range(1, width):
                gather_copy(turn, buffer, me_w - first, offset).wait_send()

    get_x.wait()
    get_down.wait()
    x = pieces[0, 0:tokens, :]
    scatter(0, jnp.dot(x, down[...], preferred_element_type=jnp.float32))
    pl.semaphore_wait(barrier, expected)
    scatter_push(0)
    fetched = [
        push(pieces.at[0, rows(0)], pieces.at[level, rows(0)], wide=me_w ^ (1 << (level - 1)))
        for level in range(1, levels + 1)
    ]
    across, aside = {}, {}

    def spread(name, buffer_slot):
        aside[name] = push(buffer_slot(0), buffer_slot(1), dp=me_d ^ 1)
        across[name] = push(buffer_slot(0), buffer_slot(2), dp=me_d ^ 2)

    def relay(name, buffer_slot):
        across[name].wait_recv()
        return push(buffer_slot(2), buffer_slot(3), dp=me_d ^ 1)

    def piece_slot(level):
        return lambda slot: pieces.at[level, rows(slot)]

    def latent_slot(slot):
        return latent.at[rows(slot)]

    def grads_slot(slot):
        return grads.at[rows(slot)]

    spread(("piece", 0), piece_slot(0))

    get_blocks.wait()
    for level in range(levels + 1):
        for block in range(halves):
            cols = pl.ds(block * block_cols, block_cols)
            keep = links[block, level].astype(jnp.float32).astype(jnp.bfloat16)
            weights[pl.ds(rank + level * features, features), cols] = (
                blocks[level, :, cols] * keep
            )

    reduce_and_gather(0, latent)

    get_up.wait()
    for level in range(1, levels + 1):
        fetched[level - 1].wait_recv()
        spread(("piece", level), piece_slot(level))
    own_pieces = jnp.concatenate(
        [pieces[level, 0:tokens, :] for level in range(levels + 1)], axis=1
    )
    base[...] = jnp.dot(own_pieces, weights[rank:, :], preferred_element_type=jnp.float32)
    get_cot.wait()

    for turn in range(2):
        half = rows(jnp.where(me_w < width // 2, turn, 1 - turn), tokens // 2)
        steps = range(turn * owners // 2, (turn + 1) * owners // 2)
        for step in steps:
            wait_chunk(0, latent, near_chunk(step))
        preact = base[half, :] + jnp.dot(
            latent[half, :], weights[0:rank, :], preferred_element_type=jnp.float32
        )
        sig = 1.0 / (1.0 + jnp.exp(-preact))
        slope = sig * (1.0 + preact * (1.0 - sig))
        grad_pre = (cot[half, :].astype(jnp.float32) * slope).astype(jnp.bfloat16)
        partial = lax.dot_general(
            grad_pre, weights[0:rank, :], (((1,), (1,)), ((), ())),
            preferred_element_type=jnp.float32,
        )
        part[half, :] = partial
        part_send[1, half, :] = partial.astype(jnp.bfloat16)
        for step in reversed(steps):
            scatter_start(1, near_chunk(step))
        grads[half, :] = grad_pre
        hidden[half, :] = (preact * sig).astype(jnp.bfloat16)
    spread("latent", latent_slot)

    def back(lo, hi):
        return lax.dot_general(
            grads[0:tokens, :], weights[lo:hi, :], (((1,), (1,)), ((), ())),
            preferred_element_type=jnp.float32,
        )

    spread("grads", grads_slot)
    contrib = back(rank, rank + (levels + 1) * features)
    for level in range(1, levels + 1):
        contrib_send[level - 1] = contrib[:, level * features:(level + 1) * features].astype(
            jnp.bfloat16
        )
    base[:, 0:features] = contrib[:, 0:features]

    relayed = [relay(("piece", level), piece_slot(level)) for level in range(levels + 1)]
    relayed.append(relay("latent", latent_slot))

    reduce_and_gather(1, mid)
    relayed.append(relay("grads", grads_slot))

    mid_spread = []

    def spread_chunk(step):
        index = near_chunk(step)
        wait_chunk(1, mid, index)
        for slot in range(1, copies):
            target = pl.ds(pl.multiple_of(slot * tokens + index * chunk, chunk), chunk)
            mid_spread.append(push(mid.at[rows(index, chunk)], mid.at[target], dp=me_d ^ slot))

    for step in range(owners // 2):
        spread_chunk(step)
    returned = [
        push(
            contrib_send.at[level - 1], contrib_got.at[level - 1], wide=me_w ^ (1 << (level - 1))
        )
        for level in range(1, levels + 1)
    ]

    def gram(left, right):
        return lax.dot_general(
            left, right, (((0,), (0,)), ((), ())), preferred_element_type=jnp.float32
        )

    for copy in aside.values():
        copy.wait_recv()
    for copy in relayed:
        copy.wait_recv()
    up_grad[...] = (scale * gram(latent[...], grads[...])).astype(jnp.bfloat16)
    for level in range(levels + 1):
        term = scale * gram(pieces[level], grads[...])
        for block in range(halves):
            cols = slice(block * block_cols, (block + 1) * block_cols)
            keep = links[block, level].astype(jnp.float32)
            block_grad[level, :, cols] = (term[:, cols] * keep).astype(jnp.bfloat16)

    for step in range(owners // 2, owners):
        spread_chunk(step)
    total = base[:, 0:features] + lax.dot_general(
        mid[0:tokens, :], down[...], (((1,), (1,)), ((), ())),
        preferred_element_type=jnp.float32,
    )
    for level in range(levels):
        returned[level].wait_recv()
        total = total + contrib_got[level].astype(jnp.float32)
    input_grad[...] = total.astype(jnp.bfloat16)
    for copy in mid_spread:
        copy.wait_recv()
    down_grad[...] = (scale * gram(pieces[0], mid[...])).astype(jnp.bfloat16)
    for copy in pending:
        copy.wait_send()
    finish(0, latent)
    finish(1, mid)


def store_kernel(*refs):
    sem = refs[-1]
    copies = [
        pltpu.make_async_copy(source, target, sem.at[i])
        for i, (source, target) in enumerate(zip(refs[:5], refs[5:10]))
    ]
    for copy in copies:
        copy.start()
    for copy in copies:
        copy.wait()


def fused(inputs, cotangent, up_blocks, block_links, rank_down, rank_up):
    width, copies = lax.axis_size("wide"), lax.axis_size("dp")
    tokens, features = inputs.shape
    level_count = up_blocks.shape[0]
    rank, units = rank_up.shape
    scale = 1.0 / math.sqrt(tokens * copies)
    levels = level_count - 1
    owners = width // 2
    chunk = tokens // owners
    remote = 2 * levels + 3 * (levels + 1) + 6 + 3 * owners
    half, full = jnp.bfloat16, jnp.float32
    shapes = (
        ((tokens, units), half), ((tokens, features), half), (up_blocks.shape, half),
        ((rank, units), half), ((features, rank), half),
    )
    anywhere = pl.BlockSpec(memory_space=pl.ANY)
    results = pl.pallas_call(
        functools.partial(fused_kernel, (width, copies, levels, scale)),
        out_shape=[pltpu.VMEM(*entry) for entry in shapes],
        in_specs=[anywhere] * 3 + [pl.BlockSpec(memory_space=pltpu.SMEM)] + [anywhere] * 2,
        out_specs=[pl.BlockSpec(memory_space=pltpu.VMEM)] * 5,
        scratch_shapes=[
            pltpu.VMEM((level_count, copies * tokens, features), half),
            pltpu.VMEM((copies * tokens, rank), half),
            pltpu.VMEM((copies * tokens, units), half),
            pltpu.VMEM((copies * tokens, rank), half),
            pltpu.VMEM((rank + level_count * features, units), half),
            pltpu.VMEM((features, rank), half),
            pltpu.VMEM((tokens, units), half),
            pltpu.VMEM(up_blocks.shape, half),
            pltpu.VMEM((tokens, rank), full),
            pltpu.VMEM((2, tokens, rank), half),
            pltpu.VMEM((2, width, chunk, rank), half),
            pltpu.VMEM((tokens, units), full),
            pltpu.VMEM((levels, tokens, features), half),
            pltpu.VMEM((levels, tokens, features), half),
            pltpu.SemaphoreType.DMA((remote,)),
            pltpu.SemaphoreType.DMA((remote,)),
            pltpu.SemaphoreType.DMA((5,)),
            pltpu.SemaphoreType.DMA((2, owners)),
            pltpu.SemaphoreType.DMA((2, width)),
            pltpu.SemaphoreType.DMA((2, width)),
            pltpu.SemaphoreType.DMA((2, owners)),
        ],
        compiler_params=pltpu.CompilerParams(collective_id=0, has_side_effects=True),
    )(inputs, cotangent, up_blocks, block_links.T, rank_down, rank_up)
    return pl.pallas_call(
        store_kernel,
        out_shape=[jax.ShapeDtypeStruct(*entry) for entry in shapes],
        in_specs=[pl.BlockSpec(memory_space=pltpu.VMEM)] * 5,
        out_specs=[pl.BlockSpec(memory_space=pltpu.HBM)] * 5,
        scratch_shapes=[pltpu.SemaphoreType.DMA((5,))],
    )(*(pltpu.with_memory_space_constraint(result, pltpu.VMEM) for result in results))


def choose(inputs, *others):
    fits = inputs.shape[0] % (TILE_ROWS * lax.axis_size("wide") // 2) == 0 and lax.axis_size("dp") == 4
    return (fused if fits else on_device)(inputs, *others)


def solution(mesh):
    in_specs = (
        P("dp", "wide"),
        P("dp", "wide"),
        P(None, None, "wide"),
        P(None, "wide"),
        P("wide", None),
        P(None, "wide"),
    )
    out_specs = (
        P("dp", "wide"),
        P("dp", "wide"),
        P(None, None, "wide"),
        P(None, "wide"),
        P("wide", None),
    )
    return jax.shard_map(
        choose, mesh=mesh, in_specs=in_specs, out_specs=out_specs, check_vma=False
    )
```
